256 devices in a mesh: ctx: 32 (over z, y), head: 8 (over x, core).
Axes of the slice: x: 4, y: 4, z: 8, core: 2. Of those that a mesh axis runs over, the one named last changes fastest.
Arguments:
- queries: bfloat16 [65536, 8, 128], P('ctx', 'head'), may hold values from -4 to 4
- keys: bfloat16 [65536, 128], P('ctx'), may hold values from -5 to 5
- values: bfloat16 [65536, 128], P('ctx'), may hold values from -6 to 6
- dout: bfloat16 [65536, 8, 128], P('ctx', 'head'), may hold values from -6 to 6
- selected: int32 [128, 3], P('ctx'), may hold values from 0 to 126, as said below
Outputs:
- grad_queries: bfloat16 [65536, 8, 128], P('ctx', 'head')
- grad_keys: bfloat16 [65536, 128], P('ctx')
- grad_values: bfloat16 [65536, 128], P('ctx')
The draws below stay inside these ranges and needn't reach their ends.
Inputs may be any that keep to these rules, and one draw needn't show every extreme that they name: `selected`: each entry of row g is either g itself, meaning no block, or an earlier block (below g); the entries of a row that are not g differ; g itself appears only in rows that have fewer than 3 earlier blocks to choose from. Over the 4 rows of one index of ctx, all entries that lie on one other index of ctx (block // 4) name the same block, so one index of ctx reads at most one block from each other index. Every row from 4 on names exactly one block among the first 4. The last row names block 126.
All inputs are finite; a program needn't handle non-finite values.
Results may differ from the reference program's by a relative error of at most 0.015.
Values may be sent and summed in bfloat16 or wider, within the bound.
A program may use at most 192 MiB of HBM per device.

```python
import math
import jax
import jax.numpy as jnp
from jax import lax

D_HEAD = 128
TOP = 3
BLK_DEV = 4
HEADS = 8
SEQ = 65536
NBLK = 128


def draw_queries(key, part):
    base_key = jax.random.fold_in(key, 21)
    result = jnp.clip(jax.random.normal(base_key, (SEQ, HEADS, D_HEAD), jnp.float32), -4.0, 4.0)
    return result.astype(jnp.bfloat16)


def draw_keys(key, part):
    base_key = jax.random.fold_in(key, 33)
    result = jnp.clip(jax.random.normal(base_key, (SEQ, D_HEAD), jnp.float32), -4.0, 4.0)
    return result.astype(jnp.bfloat16)


def draw_selected(key, part):
    blocks_all = NBLK
    devices = NBLK // BLK_DEV
    pick_key = jax.random.fold_in(key, 45)
    rank_key = jax.random.fold_in(key, 46)
    picks = jax.random.randint(pick_key, (devices, devices), 0, BLK_DEV)
    rows = jnp.arange(blocks_all, dtype=jnp.int32)
    cols = jnp.arange(blocks_all, dtype=jnp.int32)
    row_dev = rows // BLK_DEV
    col_owner = cols // BLK_DEV
    cand_hit = (cols % BLK_DEV)[None, :] == picks[row_dev[:, None], col_owner[None, :]]
    eligible = (cols[None, :] < rows[:, None]) & ((col_owner[None, :] == row_dev[:, None]) | cand_hit)
    forced = (col_owner[None, :] == 0) & cand_hit & (row_dev[:, None] >= 1)
    last_pick = (rows[:, None] == blocks_all - 1) & (cols[None, :] == blocks_all - 2)
    forced = forced | last_pick
    ranks = jax.random.randint(rank_key, (blocks_all, blocks_all), 0, 1 << 18)
    scores = ranks * blocks_all + cols[None, :] + jnp.where(forced, (1 << 18) * blocks_all, 0)
    scores = jnp.where(eligible, scores, -1)
    top_scores, top_index = lax.top_k(scores, TOP)
    chosen = jnp.where(top_scores >= 0, top_index, rows[:, None])
    return chosen.astype(jnp.int32)


def steps_of(stream_key, extent, shards, smallest, largest):
    level, own = 1.0, jax.random.fold_in(stream_key, 6)
    for position, shards_of in shards:
        draws = jnp.exp(jax.random.uniform(jax.random.fold_in(own, position), (shards_of,), jnp.float32, smallest / len(shards), largest / len(shards)))
        level = level * jnp.repeat(draws, extent[position] // shards_of).reshape([-1 if axis == position else 1 for axis in range(len(extent))])
    return level


def noise(stream_key, extent, scale, reach, split=(), kind=jnp.bfloat16):
    values = jax.random.normal(stream_key, extent, jnp.float32) * scale
    if len(split) > 0:
        values = steps_of(stream_key, extent, split, -0.22, 0.18) * values
    return jnp.clip(values, min=-reach, max=reach).astype(kind)


def setup_inputs(seed: int = 0) -> dict:
    seeds = jax.random.split(jax.random.key(seed), 6)
    queries = draw_queries(jax.random.fold_in(seeds[5], 71), 0)
    keys = draw_keys(jax.random.fold_in(seeds[5], 71), 0)
    values = noise(seeds[2], (SEQ, D_HEAD), 1.0, 6.0, ((0, 32),))
    dout = noise(seeds[3], (SEQ, HEADS, D_HEAD), 1.0, 6.0, ((0, 32), (1, 8)))
    selected = draw_selected(jax.random.fold_in(seeds[5], 71), 0)
    return dict(queries=queries, keys=keys, values=values, dout=dout, selected=selected)


def block_grads(q_rows, do_rows, key_rows, value_rows, allowed, scaling):
    scores = jnp.dot(q_rows, key_rows.T, preferred_element_type=jnp.float32) * scaling
    masked = jnp.where(allowed, scores, -jnp.inf)
    row_max = lax.optimization_barrier(jnp.max(masked, axis=1, keepdims=True))
    exp_terms = jnp.where(allowed, jnp.exp(masked - row_max), jnp.float32(0.0))
    weights = exp_terms / lax.optimization_barrier(jnp.sum(exp_terms, axis=1, keepdims=True))
    probs_b = weights.astype(jnp.bfloat16)
    attended = jnp.dot(probs_b, value_rows, preferred_element_type=jnp.float32)
    row_delta = lax.optimization_barrier(jnp.sum(do_rows.astype(jnp.float32) * attended, axis=1, keepdims=True))
    dprobs = jnp.dot(do_rows, value_rows.T, preferred_element_type=jnp.float32)
    dscores = (weights * (dprobs - row_delta)).astype(jnp.bfloat16)
    grad_q = (jnp.dot(dscores, key_rows, preferred_element_type=jnp.float32) * scaling).astype(jnp.bfloat16)
    grad_k = jnp.dot(dscores.T, q_rows, preferred_element_type=jnp.float32) * scaling
    grad_v = jnp.dot(probs_b.T, do_rows, preferred_element_type=jnp.float32)
    return (grad_q, grad_k, grad_v)

def reference(queries, keys, values, dout, selected):
    blocks_all = selected.shape[0]
    seq_rows, head_count, feature = queries.shape
    block_len = seq_rows // blocks_all
    scaling = 1.0 / math.sqrt(feature)
    key_blocks = keys.reshape(blocks_all, block_len, feature)
    value_blocks = values.reshape(blocks_all, block_len, feature)
    query_blocks = queries.reshape(blocks_all, block_len * head_count, feature)
    dout_blocks = dout.reshape(blocks_all, block_len * head_count, feature)
    row_pos = jnp.arange(block_len * head_count) // head_count
    col_pos = jnp.arange(4 * block_len)
    col_block = col_pos // block_len
    col_row = col_pos % block_len

    def per_block(running, number):
        acc_keys, acc_values = running
        entries = selected[number].astype(jnp.int32)
        alive_flags = jnp.concatenate([entries != number, jnp.ones((1,), jnp.bool_)])
        listed = jnp.concatenate([entries, number[None].astype(jnp.int32)]).astype(jnp.int32)
        allowed = jnp.where(col_block[None, :] == 3, col_row[None, :] <= row_pos[:, None], alive_flags[col_block][None, :])
        key_rows = key_blocks[listed].reshape(4 * block_len, feature)
        value_rows = value_blocks[listed].reshape(4 * block_len, feature)
        grad_q, grad_k, grad_v = block_grads(query_blocks[number], dout_blocks[number], key_rows, value_rows, allowed, scaling)
        acc_keys = acc_keys.at[listed].add(grad_k.reshape(4, block_len, feature))
        acc_values = acc_values.at[listed].add(grad_v.reshape(4, block_len, feature))
        return ((acc_keys, acc_values), grad_q)
    start = jnp.zeros((blocks_all, block_len, feature), jnp.float32)
    (acc_keys, acc_values), grads_q = lax.scan(per_block, (start, start), jnp.arange(blocks_all, dtype=jnp.int32))
    grad_queries = grads_q.reshape(seq_rows, head_count, feature)
    grad_keys = acc_keys.reshape(seq_rows, feature).astype(jnp.bfloat16)
    grad_values = acc_values.reshape(seq_rows, feature).astype(jnp.bfloat16)
    return (grad_queries, grad_keys, grad_values)
```

```python
import functools
import math

import jax
import jax.numpy as jnp
from jax import lax
from jax.experimental import pallas as pl
from jax.experimental.pallas import tpu as pltpu
from jax.sharding import PartitionSpec as P

MESH = pl.DeviceIdType.MESH
F32 = jnp.float32
BF16 = jnp.bfloat16
VM = pl.BlockSpec(memory_space=pltpu.VMEM)
SM = pl.BlockSpec(memory_space=pltpu.SMEM)


def greet(n):
    me = lax.axis_index("ctx")
    head = lax.axis_index("head")
    chip, core = head // 2, head % 2
    barrier = pltpu.get_barrier_semaphore()

    def hello(step, carry):
        pl.semaphore_signal(
            barrier, inc=1, device_id={"ctx": lax.rem(me + step, n)}, device_id_type=MESH
        )
        return carry

    lax.fori_loop(1, n, hello, 0)
    for step in range(1, 4):
        pl.semaphore_signal(
            barrier,
            inc=1,
            device_id={"head": lax.rem(chip + step, 4) * 2 + core},
            device_id_type=MESH,
        )
    pl.semaphore_signal(
        barrier, inc=1, device_id={"head": chip * 2 + 1 - core}, device_id_type=MESH
    )
    pl.semaphore_wait(barrier, n - 1 + 4)
    return me, chip, core


def fetch_kernel(
    n,
    cidx,
    ask,
    keys,
    values,
    queries,
    dout,
    q_out,
    do_out,
    kv_out,
    asked,
    table,
    send,
    comp,
    ask_send,
    ask_recv,
    kv_send,
    kv_recv,
    x_send,
    x_recv,
    core_send,
    core_recv,
):
    rows = keys.shape[2]
    me, chip, core = greet(n)

    def to_chip(step, slot, src, dst):
        peer = lax.rem(chip + step, 4)
        return pltpu.make_async_remote_copy(
            src_ref=src(peer),
            dst_ref=dst,
            send_sem=x_send.at[slot, step],
            recv_sem=x_recv.at[slot, step],
            device_id={"head": peer * 2 + core},
            device_id_type=MESH,
        )

    def ask_copy(owner, place):
        return pltpu.make_async_remote_copy(
            src_ref=ask.at[owner],
            dst_ref=asked.at[place],
            send_sem=ask_send.at[owner],
            recv_sem=ask_recv.at[place],
            device_id={"ctx": owner},
            device_id_type=MESH,
        )

    def kv_copy(reader, place):
        return pltpu.make_async_remote_copy(
            src_ref=send.at[reader],
            dst_ref=table.at[place],
            send_sem=kv_send.at[reader],
            recv_sem=kv_recv.at[place],
            device_id={"ctx": reader},
            device_id_type=MESH,
        )

    def start_ask(owner, carry):
        ask_copy(owner, me).start()
        return carry

    lax.fori_loop(0, me, start_ask, 0)
    q_copies = []
    for step in (1, 3, 2):
        q_copies.append(to_chip(step, 0, lambda peer: queries.at[peer], q_out.at[chip]))
        q_copies.append(to_chip(step, 1, lambda peer: dout.at[peer], do_out.at[chip]))
    for copy in q_copies:
        copy.start()
    q_out[chip] = queries[chip]
    do_out[chip] = dout[chip]
    part = core * 4 + chip
    for b in range(4):
        table[n + b, 0] = keys[b, part]
        table[n + b, 1] = values[b, part]

    def serve(reader, carry):
        ask_copy(reader, reader).wait_recv()
        wish = asked[reader].astype(F32)
        masks = [jnp.where(wish == b, 1.0, 0.0).astype(BF16) for b in range(4)]
        for half in range(2):
            for g in range(rows // 16):
                span = pl.ds(16 * g, 16)
                total = table[n, half, span] * masks[0]
                for b in range(1, 4):
                    total = total + table[n + b, half, span] * masks[b]
                send[reader, half, span] = total
        kv_copy(reader, me).start()
        return carry

    lax.fori_loop(me + 1, n, serve, 0)

    def got_kv(owner, carry):
        kv_copy(owner, owner).wait_recv()
        return carry

    lax.fori_loop(0, me, got_kv, 0)

    for x in range(4):
        for t in range(3):
            comp[x, t] = table[cidx[x * 3 + t]]
    kv_copies = [
        to_chip(step, 2, lambda peer: comp.at[peer], kv_out.at[:, :, core, chip])
        for step in (1, 3, 2)
    ]
    for copy in kv_copies:
        copy.start()
    for t in range(3):
        for half in range(2):
            kv_out[t, half, core, chip] = comp[chip, t, half]
    for copy in kv_copies:
        copy.wait_recv()
    swap = pltpu.make_async_remote_copy(
        src_ref=kv_out.at[:, :, core],
        dst_ref=kv_out.at[:, :, core],
        send_sem=core_send,
        recv_sem=core_recv,
        device_id={"head": chip * 2 + 1 - core},
        device_id_type=MESH,
    )
    swap.start()
    for copy in q_copies:
        copy.wait()
    for copy in kv_copies:
        copy.wait_send()

    def sent_ask(owner, carry):
        ask_copy(owner, me).wait_send()
        return carry

    lax.fori_loop(0, me, sent_ask, 0)

    def sent_kv(reader, carry):
        kv_copy(reader, me).wait_send()
        return carry

    lax.fori_loop(me + 1, n, sent_kv, 0)
    swap.wait()


def attend_kernel(
    scaling, meta, q_ref, do_ref, kv_ref, k_own, v_own, gq_ref, terms, scores, dprobs, acc, k_turned
):
    head = pl.program_id(0)
    length = q_ref.shape[1]
    factor = scaling * math.log2(math.e)
    nt = (((1,), (1,)), ((), ()))

    def key_rows(t):
        return kv_ref[t, 0] if t < 3 else k_own[0]

    def value_rows(t):
        return kv_ref[t, 1] if t < 3 else v_own[0]

    @pl.when(head == 0)
    def _():
        acc[...] = jnp.zeros_like(acc)
        for t in range(4):
            k_turned[t] = key_rows(t).T

    q = q_ref[0]
    do = do_ref[0]
    live = [meta[t] > 0 for t in range(3)]
    top = None
    for t in range(4):
        s = lax.dot_general(key_rows(t), q, nt, preferred_element_type=F32)
        if t == 3:
            col = lax.broadcasted_iota(jnp.int32, (length, length), 0)
            row = lax.broadcasted_iota(jnp.int32, (length, length), 1)
            s = jnp.where(col <= row, s, -jnp.inf)
        scores[t] = s
        best = jnp.max(s, axis=0, keepdims=True)
        if t < 3:
            best = jnp.where(live[t], best, -jnp.inf)
        top = best if top is None else jnp.maximum(top, best)
    top = top * factor
    total = jnp.zeros((1, length), F32)
    weighted = jnp.zeros((1, length), F32)
    for t in range(4):
        shift = jnp.where(live[t], top, jnp.inf) if t < 3 else top
        e = jnp.exp2(scores[t] * factor - shift)
        dp = lax.dot_general(value_rows(t), do, nt, preferred_element_type=F32)
        total = total + jnp.sum(e, axis=0, keepdims=True)
        weighted = weighted + jnp.sum(e * dp, axis=0, keepdims=True)
        scores[t] = e
        dprobs[t] = dp
    inverse = 1.0 / total
    delta = weighted * inverse
    gq = jnp.zeros((q.shape[1], length), F32)
    for t in range(4):
        p = scores[t] * inverse
        ds = (p * (dprobs[t] - delta)).astype(BF16)
        acc[t, 1] += jnp.dot(p.astype(BF16), do, preferred_element_type=F32)
        acc[t, 0] += jnp.dot(ds, q, preferred_element_type=F32)
        gq = gq + jnp.dot(k_turned[t], ds, preferred_element_type=F32)
    gq_ref[0] = (gq * scaling).T.astype(BF16)

    @pl.when(head == pl.num_programs(0) - 1)
    def _():
        for t in range(4):
            terms[t, 0] = (acc[t, 0] * scaling).astype(BF16)
            terms[t, 1] = acc[t, 1].astype(BF16)


def return_kernel(
    n,
    tix,
    terms,
    gq,
    asked,
    gq_out,
    gk_out,
    gv_out,
    pair,
    outgoing,
    incoming,
    send,
    back,
    own,
    final,
    back_send,
    back_recv,
    x_send,
    x_recv,
    core_send,
    core_recv,
):
    rows = terms.shape[4]
    me, chip, core = greet(n)

    def to_chip(step, slot, src, dst):
        peer = lax.rem(chip + step, 4)
        return pltpu.make_async_remote_copy(
            src_ref=src(peer),
            dst_ref=dst,
            send_sem=x_send.at[slot, step],
            recv_sem=x_recv.at[slot, step],
            device_id={"head": peer * 2 + core},
            device_id_type=MESH,
        )

    def to_core(slot, src, dst):
        return pltpu.make_async_remote_copy(
            src_ref=src,
            dst_ref=dst,
            send_sem=core_send.at[slot],
            recv_sem=core_recv.at[slot],
            device_id={"head": chip * 2 + 1 - core},
            device_id_type=MESH,
        )

    def back_copy(owner, place):
        return pltpu.make_async_remote_copy(
            src_ref=send.at[owner],
            dst_ref=back.at[place],
            send_sem=back_send.at[owner],
            recv_sem=back_recv.at[place],
            device_id={"ctx": owner},
            device_id_type=MESH,
        )

    merge = to_core(0, terms.at[:, :, 1 - core], pair)
    merge.start()
    for x in range(4):
        incoming[x, 4] = jnp.zeros_like(incoming[x, 4])
    merge.wait()
    for t in range(4):
        for half in range(2):
            for x in range(4):
                total = terms[t, half, core, x].astype(F32) + pair[t, half, x].astype(F32)
                outgoing[x, t, half] = total.astype(BF16)
    spread = [
        to_chip(step, 0, lambda peer: outgoing.at[peer], incoming.at[chip, pl.ds(0, 4)])
        for step in (1, 3, 2)
    ]
    for copy in spread:
        copy.start()
    for t in range(4):
        incoming[chip, t] = outgoing[chip, t]
    gq_copies = [
        to_chip(step, 1, lambda peer: gq.at[peer], gq_out.at[chip]) for step in (1, 3, 2)
    ]
    for copy in spread:
        copy.wait_recv()

    def collect(place):
        total = incoming[0, tix[place]].astype(F32)
        for x in range(1, 4):
            total = total + incoming[x, tix[x * (n + 4) + place]].astype(F32)
        return total

    def give_back(owner, carry):
        send[owner] = collect(owner).astype(BF16)
        back_copy(owner, me).start()
        return carry

    lax.fori_loop(0, me, give_back, 0)
    for copy in gq_copies:
        copy.start()
    gq_out[chip] = gq[chip]
    for b in range(4):
        own[b] = collect(n + b)

    def take_back(reader, carry):
        back_copy(reader, reader).wait_recv()
        wish = asked[reader].astype(F32)
        masks = [jnp.where(wish == b, 1.0, 0.0) for b in range(4)]
        for half in range(2):
            for g in range(rows // 16):
                span = pl.ds(16 * g, 16)
                part = back[reader, half, span].astype(F32)
                for b in range(4):
                    own[b, half, span] += part * masks[b]
        return carry

    lax.fori_loop(me + 1, n, take_back, 0)
    for b in range(4):
        final[0, b] = own[b, 0].astype(BF16)
        final[1, b] = own[b, 1].astype(BF16)
    shares = []
    for step in (1, 3, 2):
        shares.append(to_chip(step, 2, lambda peer: final.at[0], gk_out.at[:, core, chip]))
        shares.append(to_chip(step, 3, lambda peer: final.at[1], gv_out.at[:, core, chip]))
    for copy in shares:
        copy.start()
    for b in range(4):
        gk_out[b, core, chip] = final[0, b]
        gv_out[b, core, chip] = final[1, b]
    for copy in shares:
        copy.wait_recv()
    swap_k = to_core(1, gk_out.at[:, core], gk_out.at[:, core])
    swap_v = to_core(2, gv_out.at[:, core], gv_out.at[:, core])
    swap_k.start()
    swap_v.start()
    for copy in shares + spread:
        copy.wait_send()
    for copy in gq_copies:
        copy.wait()

    def sent_back(owner, carry):
        back_copy(owner, me).wait_send()
        return carry

    lax.fori_loop(0, me, sent_back, 0)
    swap_k.wait()
    swap_v.wait()


def body(queries, keys, values, dout, selected):
    tok, _, feature = queries.shape
    blocks = selected.shape[0]
    length = tok // blocks
    rows = length // 8
    n = lax.axis_size("ctx")
    me = lax.axis_index("ctx")
    chip = lax.axis_index("head") // 2
    scaling = 1.0 / math.sqrt(feature)
    dma = pltpu.SemaphoreType.DMA

    local = jnp.arange(blocks, dtype=jnp.int32)
    vacant = selected == (me * blocks + local)[:, None]
    owners = selected // blocks
    inside = selected % blocks
    distant = (owners != me) & jnp.logical_not(vacant)
    near = (owners == me) & jnp.logical_not(vacant)
    peers = jnp.arange(n, dtype=jnp.int32)
    hits = distant[:, :, None] & (owners[:, :, None] == peers)
    wanted = jnp.max(jnp.where(hits, inside[:, :, None], -1), axis=(0, 1))
    ask = jnp.broadcast_to(wanted.astype(BF16)[:, None, None], (n, 16, 128))
    cidx = jnp.where(vacant, n + local[:, None], jnp.where(owners == me, n + inside, owners))
    near_hits = near[:, :, None] & (inside[:, :, None] == local)
    tcol = jnp.arange(3, dtype=jnp.int32)[None, :, None]
    far_t = jnp.min(jnp.where(hits, tcol, 4), axis=1)
    near_t = jnp.min(jnp.where(near_hits, tcol, 4), axis=1)
    near_t = jnp.where(local[:, None] == local[None, :], 3, near_t)
    tix = jnp.concatenate([far_t, near_t], axis=1).reshape(-1)
    alive = lax.dynamic_index_in_dim(
        jnp.logical_not(vacant).astype(jnp.int32), chip, 0, keepdims=False
    )
    meta = jnp.concatenate([alive, chip.astype(jnp.int32)[None]])

    q_blocks = queries.reshape(blocks, length, feature)
    do_blocks = dout.reshape(blocks, length, feature)
    k_blocks = keys.reshape(blocks, length, feature)
    v_blocks = values.reshape(blocks, length, feature)
    heads_shape = jax.ShapeDtypeStruct((4, length, feature), BF16)
    q_mine, do_mine, kv_list, asked = pl.pallas_call(
        functools.partial(fetch_kernel, n),
        out_shape=(
            heads_shape,
            heads_shape,
            jax.ShapeDtypeStruct((3, 2, 2, 4, rows, feature), BF16),
            jax.ShapeDtypeStruct((n, 16, 128), BF16),
        ),
        in_specs=[SM, VM, VM, VM, VM, VM],
        out_specs=(VM, VM, VM, VM),
        scratch_shapes=[
            pltpu.VMEM((n + 4, 2, rows, feature), BF16),
            pltpu.VMEM((n, 2, rows, feature), BF16),
            pltpu.VMEM((4, 3, 2, rows, feature), BF16),
            dma((n,)),
            dma((n,)),
            dma((n,)),
            dma((n,)),
            dma((3, 4)),
            dma((3, 4)),
            dma,
            dma,
        ],
        compiler_params=pltpu.CompilerParams(collective_id=0, has_side_effects=True),
        name="fetch",
    )(
        cidx.reshape(-1),
        ask,
        k_blocks.reshape(blocks, 8, rows, feature),
        v_blocks.reshape(blocks, 8, rows, feature),
        q_blocks,
        do_blocks,
    )
    kv_list = kv_list.reshape(3, 2, length, feature)
    per_head = pl.BlockSpec((1, length, feature), lambda h, m: (h, 0, 0))
    own_block = pl.BlockSpec((1, length, feature), lambda h, m: (m[3], 0, 0))
    gq_mine, terms = pl.pallas_call(
        functools.partial(attend_kernel, scaling),
        out_shape=(heads_shape, jax.ShapeDtypeStruct((4, 2, length, feature), BF16)),
        grid_spec=pltpu.PrefetchScalarGridSpec(
            num_scalar_prefetch=1,
            grid=(4,),
            in_specs=[
                per_head,
                per_head,
                pl.BlockSpec((3, 2, length, feature), lambda h, m: (0, 0, 0, 0)),
                own_block,
                own_block,
            ],
            out_specs=[
                per_head,
                pl.BlockSpec((4, 2, length, feature), lambda h, m: (0, 0, 0, 0)),
            ],
            scratch_shapes=[
                pltpu.VMEM((4, length, length), F32),
                pltpu.VMEM((4, length, length), F32),
                pltpu.VMEM((4, 2, length, feature), F32),
                pltpu.VMEM((4, feature, length), BF16),
            ],
        ),
        compiler_params=pltpu.CompilerParams(vmem_limit_bytes=56 * 2**20),
        name="attend",
    )(meta, q_mine, do_mine, kv_list, k_blocks, v_blocks)
    part_shape = jax.ShapeDtypeStruct((blocks, 2, 4, rows, feature), BF16)
    gq, gk, gv = pl.pallas_call(
        functools.partial(return_kernel, n),
        out_shape=(heads_shape, part_shape, part_shape),
        in_specs=[SM, VM, VM, VM],
        out_specs=(VM, VM, VM),
        scratch_shapes=[
            pltpu.VMEM((4, 2, 4, rows, feature), BF16),
            pltpu.VMEM((4, 4, 2, rows, feature), BF16),
            pltpu.VMEM((4, 5, 2, rows, feature), BF16),
            pltpu.VMEM((n, 2, rows, feature), BF16),
            pltpu.VMEM((n, 2, rows, feature), BF16),
            pltpu.VMEM((4, 2, rows, feature), F32),
            pltpu.VMEM((2, 4, rows, feature), BF16),
            dma((n,)),
            dma((n,)),
            dma((4, 4)),
            dma((4, 4)),
            dma((3,)),
            dma((3,)),
        ],
        compiler_params=pltpu.CompilerParams(collective_id=1, has_side_effects=True),
        name="give_back",
    )(tix, terms.reshape(4, 2, 2, 4, rows, feature), gq_mine, asked)
    return (
        gq.reshape(queries.shape),
        gk.reshape(keys.shape),
        gv.reshape(values.shape),
    )


def solution(mesh):
    return jax.shard_map(
        body,
        mesh=mesh,
        in_specs=(
            P("ctx", "head", None),
            P("ctx", None),
            P("ctx", None),
            P("ctx", "head", None),
            P("ctx", None),
        ),
        out_specs=(P("ctx", "head", None), P("ctx", None), P("ctx", None)),
        check_vma=False,
    )
```

```python
import functools
import math

import jax
import jax.numpy as jnp
from jax import lax
from jax.experimental import pallas as pl
from jax.experimental.pallas import tpu as pltpu
from jax.sharding import PartitionSpec as P

MESH = pl.DeviceIdType.MESH
F32 = jnp.float32
BF16 = jnp.bfloat16
VM = pl.BlockSpec(memory_space=pltpu.VMEM)
SM = pl.BlockSpec(memory_space=pltpu.SMEM)


def place():
    me = lax.axis_index("ctx")
    head = lax.axis_index("head")
    return me // 4, me % 4, head // 2, head % 2


def greet(nz):
    z, y, chip, core = place()
    barrier = pltpu.get_barrier_semaphore()

    def hello(**where):
        pl.semaphore_signal(barrier, inc=1, device_id=where, device_id_type=MESH)

    hello(ctx=lax.rem(z + 1, nz) * 4 + y)
    hello(ctx=lax.rem(z + nz - 1, nz) * 4 + y)
    for step in range(1, 4):
        hello(ctx=z * 4 + lax.rem(y + step, 4))
        hello(head=lax.rem(chip + step, 4) * 2 + core)
    hello(head=chip * 2 + 1 - core)
    pl.semaphore_wait(barrier, 9)
    return z, y, chip, core


def fetch_kernel(
    nz,
    cidx,
    ask,
    keys,
    values,
    queries,
    dout,
    q_out,
    do_out,
    kv_out,
    asked,
    pool,
    send,
    comp,
    ask_send,
    ask_recv,
    z_send,
    z_recv,
    y_send,
    y_recv,
    x_send,
    x_recv,
    core_send,
    core_recv,
):
    rows = keys.shape[2]
    reach = nz // 2
    wrap = nz - 1 - reach
    z, y, chip, core = greet(nz)
    part = core * 4 + chip

    def to_chip(step, slot, src, dst):
        peer = lax.rem(chip + step, 4)
        return pltpu.make_async_remote_copy(
            src_ref=src(peer),
            dst_ref=dst,
            send_sem=x_send.at[slot, step],
            recv_sem=x_recv.at[slot, step],
            device_id={"head": peer * 2 + core},
            device_id_type=MESH,
        )

    def ask_copy(step):
        peer = lax.rem(y + step, 4)
        return pltpu.make_async_remote_copy(
            src_ref=ask.at[peer],
            dst_ref=asked.at[y],
            send_sem=ask_send.at[step],
            recv_sem=ask_recv.at[step],
            device_id={"ctx": z * 4 + peer},
            device_id_type=MESH,
        )

    def relay(source, half, back, hop):
        there = pool.at[pl.ds(4 * source, 4), half]
        if hop == 1:
            here = (keys, values)[half].at[:, part]
        else:
            here = there
        peer = lax.rem(z + nz - 1, nz) if back else lax.rem(z + 1, nz)
        return pltpu.make_async_remote_copy(
            src_ref=here,
            dst_ref=there,
            send_sem=z_send.at[back, hop - 1, half],
            recv_sem=z_recv.at[source, half],
            device_id={"ctx": peer * 4 + y},
            device_id_type=MESH,
        )

    def forward_source(hop):
        return z - hop + 1, jnp.logical_and(z <= nz - 2, z >= hop - 1)

    def backward_source(hop):
        source = lax.rem(z + hop - 1, nz)
        return source, source <= wrap - 1

    def start_relay(back, hop, half):
        source, needed = (backward_source if back else forward_source)(hop)

        @pl.when(needed)
        def _():
            relay(source, half, back, hop).start()

    def slot_copy(step, source):
        peer = lax.rem(y + step, 4)
        return pltpu.make_async_remote_copy(
            src_ref=send.at[step - 1, source],
            dst_ref=pool.at[4 * nz + 4 * source + y],
            send_sem=y_send.at[step - 1, source],
            recv_sem=y_recv.at[step - 1, source],
            device_id={"ctx": z * 4 + peer},
            device_id_type=MESH,
        )

    def serve(source):
        for step in range(1, 4):
            peer = lax.rem(y + step, 4)
            wish = jnp.broadcast_to(asked[peer, pl.ds(source, 1)], (16, 128))
            masks = [jnp.where(wish == b, 1.0, 0.0).astype(BF16) for b in range(4)]
            for half in range(2):
                for g in range(rows // 16):
                    span = pl.ds(16 * g, 16)
                    total = pool[4 * source, half, span] * masks[0]
                    for b in range(1, 4):
                        total = total + pool[4 * source + b, half, span] * masks[b]
                    send[step - 1, source, half, span] = total
        for step in range(1, 4):
            slot_copy(step, source).start()

    asks = [ask_copy(step) for step in range(1, 4)]
    for copy in asks:
        copy.start()
    for half in range(2):
        start_relay(0, 1, half)
        start_relay(1, 1, half)
    q_copies = []
    for step in (1, 3, 2):
        q_copies.append(to_chip(step, 0, lambda peer: queries.at[peer], q_out.at[chip]))
        q_copies.append(to_chip(step, 1, lambda peer: dout.at[peer], do_out.at[chip]))
    for copy in q_copies:
        copy.start()
    for b in range(4):
        pool[4 * z + b, 0] = keys[b, part]
        pool[4 * z + b, 1] = values[b, part]
    asked[y] = ask[y]
    for copy in asks:
        copy.wait_recv()
    serve(z)
    q_out[chip] = queries[chip]
    do_out[chip] = dout[chip]
    for hop in range(1, reach + 1):
        near = z - hop
        far = lax.rem(z + hop, nz)
        for half in range(2):

            @pl.when(near >= 0)
            def _():
                relay(near, half, 0, 2).wait_recv()

            if hop < reach:
                start_relay(0, hop + 1, half)
            if hop <= wrap:

                @pl.when(far <= wrap - 1)
                def _():
                    relay(far, half, 1, 2).wait_recv()

                if hop < wrap:
                    start_relay(1, hop + 1, half)

        @pl.when(near >= 0)
        def _():
            serve(near)

        if hop <= wrap:

            @pl.when(jnp.logical_and(far <= wrap - 1, far < z))
            def _():
                serve(far)

    def got_slots(source, carry):
        for step in range(1, 4):
            slot_copy(step, source).wait_recv()
        return carry

    lax.fori_loop(0, z + 1, got_slots, 0)

    for x in range(4):
        for t in range(3):
            comp[x, t] = pool[cidx[x * 3 + t]]
    kv_copies = [
        to_chip(step, 2, lambda peer: comp.at[peer], kv_out.at[:, :, core, chip])
        for step in (1, 3, 2)
    ]
    for copy in kv_copies:
        copy.start()
    for t in range(3):
        for half in range(2):
            kv_out[t, half, core, chip] = comp[chip, t, half]
    for copy in kv_copies:
        copy.wait_recv()
    swap = pltpu.make_async_remote_copy(
        src_ref=kv_out.at[:, :, core],
        dst_ref=kv_out.at[:, :, core],
        send_sem=core_send,
        recv_sem=core_recv,
        device_id={"head": chip * 2 + 1 - core},
        device_id_type=MESH,
    )
    swap.start()
    for copy in q_copies:
        copy.wait()
    for copy in kv_copies + asks:
        copy.wait_send()
    for back, last in ((0, reach), (1, wrap)):
        for hop in range(1, last + 1):
            source, needed = (backward_source if back else forward_source)(hop)
            for half in range(2):

                @pl.when(needed)
                def _():
                    relay(source, half, back, hop).wait_send()

    def sent_slots(source, carry):
        for step in range(1, 4):
            slot_copy(step, source).wait_send()
        return carry

    lax.fori_loop(0, z + 1, sent_slots, 0)
    swap.wait()


def attend_kernel(
    scaling, meta, q_ref, do_ref, kv_ref, k_own, v_own, gq_ref, terms, scores, dprobs, acc, k_turned
):
    head = pl.program_id(0)
    length = q_ref.shape[1]
    factor = scaling * math.log2(math.e)
    nt = (((1,), (1,)), ((), ()))

    def key_rows(t):
        return kv_ref[t, 0] if t < 3 else k_own[0]

    def value_rows(t):
        return kv_ref[t, 1] if t < 3 else v_own[0]

    @pl.when(head == 0)
    def _():
        acc[...] = jnp.zeros_like(acc)
        for t in range(4):
            k_turned[t] = key_rows(t).T

    q = q_ref[0]
    do = do_ref[0]
    live = [meta[t] > 0 for t in range(3)]
    top = None
    for t in range(4):
        s = lax.dot_general(key_rows(t), q, nt, preferred_element_type=F32)
        if t == 3:
            col = lax.broadcasted_iota(jnp.int32, (length, length), 0)
            row = lax.broadcasted_iota(jnp.int32, (length, length), 1)
            s = jnp.where(col <= row, s, -jnp.inf)
        scores[t] = s
        best = jnp.max(s, axis=0, keepdims=True)
        if t < 3:
            best = jnp.where(live[t], best, -jnp.inf)
        top = best if top is None else jnp.maximum(top, best)
    top = top * factor
    total = jnp.zeros((1, length), F32)
    weighted = jnp.zeros((1, length), F32)
    for t in range(4):
        shift = jnp.where(live[t], top, jnp.inf) if t < 3 else top
        e = jnp.exp2(scores[t] * factor - shift)
        dp = lax.dot_general(value_rows(t), do, nt, preferred_element_type=F32)
        total = total + jnp.sum(e, axis=0, keepdims=True)
        weighted = weighted + jnp.sum(e * dp, axis=0, keepdims=True)
        scores[t] = e
        dprobs[t] = dp
    inverse = 1.0 / total
    delta = weighted * inverse
    gq = jnp.zeros((q.shape[1], length), F32)
    for t in range(4):
        p = scores[t] * inverse
        ds = (p * (dprobs[t] - delta)).astype(BF16)
        acc[t, 1] += jnp.dot(p.astype(BF16), do, preferred_element_type=F32)
        acc[t, 0] += jnp.dot(ds, q, preferred_element_type=F32)
        gq = gq + jnp.dot(k_turned[t], ds, preferred_element_type=F32)
    gq_ref[0] = (gq * scaling).T.astype(BF16)

    @pl.when(head == pl.num_programs(0) - 1)
    def _():
        for t in range(4):
            terms[t, 0] = (acc[t, 0] * scaling).astype(BF16)
            terms[t, 1] = acc[t, 1].astype(BF16)


def return_kernel(
    nz,
    tix,
    terms,
    gq,
    asked,
    gq_out,
    gk_out,
    gv_out,
    pair,
    outgoing,
    incoming,
    y_out,
    y_in,
    sums,
    z_out,
    z_in,
    final,
    y_send,
    y_recv,
    z_send,
    z_recv,
    x_send,
    x_recv,
    core_send,
    core_recv,
):
    rows = terms.shape[4]
    n = 4 * nz
    reach = nz // 2
    wrap = nz - 1 - reach
    z, y, chip, core = greet(nz)

    def to_chip(step, slot, src, dst):
        peer = lax.rem(chip + step, 4)
        return pltpu.make_async_remote_copy(
            src_ref=src(peer),
            dst_ref=dst,
            send_sem=x_send.at[slot, step],
            recv_sem=x_recv.at[slot, step],
            device_id={"head": peer * 2 + core},
            device_id_type=MESH,
        )

    def to_core(slot, src, dst):
        return pltpu.make_async_remote_copy(
            src_ref=src,
            dst_ref=dst,
            send_sem=core_send.at[slot],
            recv_sem=core_recv.at[slot],
            device_id={"head": chip * 2 + 1 - core},
            device_id_type=MESH,
        )

    def slot_copy(step, owner):
        return pltpu.make_async_remote_copy(
            src_ref=y_out.at[step, owner],
            dst_ref=y_in.at[step, owner],
            send_sem=y_send.at[step, owner],
            recv_sem=y_recv.at[step, owner],
            device_id={"ctx": z * 4 + lax.rem(y + step, 4)},
            device_id_type=MESH,
        )

    def relay(owner, half, back):
        peer = lax.rem(z + 1, nz) if back else lax.rem(z + nz - 1, nz)
        return pltpu.make_async_remote_copy(
            src_ref=z_out.at[owner, half],
            dst_ref=z_in.at[back, owner, half],
            send_sem=z_send.at[owner, half],
            recv_sem=z_recv.at[back, owner, half],
            device_id={"ctx": peer * 4 + y},
            device_id_type=MESH,
        )

    merge = to_core(0, terms.at[:, :, 1 - core], pair)
    merge.start()
    for x in range(4):
        incoming[x, 4] = jnp.zeros_like(incoming[x, 4])
    for owner in range(nz):
        sums[owner] = jnp.zeros_like(sums[owner])
    merge.wait()
    for t in range(4):
        for half in range(2):
            for x in range(4):
                total = terms[t, half, core, x].astype(F32) + pair[t, half, x].astype(F32)
                outgoing[x, t, half] = total.astype(BF16)
    spread = [
        to_chip(step, 0, lambda peer: outgoing.at[peer], incoming.at[chip, pl.ds(0, 4)])
        for step in (1, 3, 2)
    ]
    for copy in spread:
        copy.start()
    for t in range(4):
        incoming[chip, t] = outgoing[chip, t]
    gq_copies = [
        to_chip(step, 1, lambda peer: gq.at[peer], gq_out.at[chip]) for step in (1, 3, 2)
    ]
    for copy in spread:
        copy.wait_recv()

    def collect(place):
        total = incoming[0, tix[place]].astype(F32)
        for x in range(1, 4):
            total = total + incoming[x, tix[x * (n + 4) + place]].astype(F32)
        return total

    def give(owner):
        for step in range(4):
            y_out[step, owner] = collect(4 * owner + lax.rem(y + step, 4)).astype(BF16)
        for step in range(1, 4):
            slot_copy(step, owner).start()

    def gather(owner):
        for step in range(1, 4):
            slot_copy(step, owner).wait_recv()
        masks = []
        for step in range(4):
            wish = jnp.broadcast_to(asked[lax.rem(y + 4 - step, 4), pl.ds(owner, 1)], (16, 128))
            masks.append([jnp.where(wish == b, 1.0, 0.0) for b in range(4)])
        for half in range(2):
            for g in range(rows // 16):
                span = pl.ds(16 * g, 16)
                parts = [y_out[0, owner, half, span].astype(F32)]
                for step in range(1, 4):
                    parts.append(y_in[step, owner, half, span].astype(F32))
                for b in range(4):
                    total = parts[0] * masks[0][b]
                    for step in range(1, 4):
                        total = total + parts[step] * masks[step][b]
                    sums[owner, half, b, span] = total

    def pass_on(owner, half, back, last):
        if last:
            z_out[owner, half] = sums[owner, half].astype(BF16)
        elif back:
            relay(owner, half, back).wait_recv()
            z_out[owner, half] = (
                sums[owner, half] + z_in[back, owner, half].astype(F32)
            ).astype(BF16)
        else:

            @pl.when(z <= nz - 2)
            def _():
                relay(owner, half, back).wait_recv()
                z_out[owner, half] = (
                    sums[owner, half] + z_in[back, owner, half].astype(F32)
                ).astype(BF16)

            @pl.when(z == nz - 1)
            def _():
                z_out[owner, half] = sums[owner, half].astype(BF16)

        relay(owner, half, back).start()

    steps = []
    for i in range(reach):
        near = z - (reach - i)
        steps.append((near, near >= 0, near >= 0, 0, i == 0))
        if i < wrap:
            far = lax.rem(z + wrap - i, nz)
            needed = far <= wrap - 1
            steps.append((far, needed, jnp.logical_and(needed, far < z), 1, i == 0))
    for owner, _, mine, _, _ in steps:

        @pl.when(mine)
        def _():
            give(owner)

    give(z)
    for copy in gq_copies:
        copy.start()
    gq_out[chip] = gq[chip]
    for owner, needed, mine, back, last in steps:

        @pl.when(mine)
        def _():
            gather(owner)

        @pl.when(needed)
        def _():
            for half in range(2):
                pass_on(owner, half, back, last)

    gather(z)
    for b in range(4):
        near_sum = collect(n + b)
        for half in range(2):
            sums[z, half, b] += near_sum[half]
    for half in range(2):

        @pl.when(z <= nz - 2)
        def _():
            relay(z, half, 0).wait_recv()
            sums[z, half] += z_in[0, z, half].astype(F32)

        @pl.when(z <= wrap - 1)
        def _():
            relay(z, half, 1).wait_recv()
            sums[z, half] += z_in[1, z, half].astype(F32)

        final[half] = sums[z, half].astype(BF16)
    shares = []
    for step in (1, 3, 2):
        shares.append(to_chip(step, 2, lambda peer: final.at[0], gk_out.at[:, core, chip]))
        shares.append(to_chip(step, 3, lambda peer: final.at[1], gv_out.at[:, core, chip]))
    for copy in shares:
        copy.start()
    for b in range(4):
        gk_out[b, core, chip] = final[0, b]
        gv_out[b, core, chip] = final[1, b]
    for copy in shares:
        copy.wait_recv()
    swap_k = to_core(1, gk_out.at[:, core], gk_out.at[:, core])
    swap_v = to_core(2, gv_out.at[:, core], gv_out.at[:, core])
    swap_k.start()
    swap_v.start()
    for copy in shares + spread:
        copy.wait_send()
    for copy in gq_copies:
        copy.wait()
    for owner, needed, _, back, _ in steps:

        @pl.when(needed)
        def _():
            for half in range(2):
                relay(owner, half, back).wait_send()

    def sent_slots(owner, carry):
        for step in range(1, 4):
            slot_copy(step, owner).wait_send()
        return carry

    lax.fori_loop(0, z + 1, sent_slots, 0)
    swap_k.wait()
    swap_v.wait()


def body(queries, keys, values, dout, selected):
    tok, _, feature = queries.shape
    blocks = selected.shape[0]
    length = tok // blocks
    rows = length // 8
    n = lax.axis_size("ctx")
    me = lax.axis_index("ctx")
    chip = lax.axis_index("head") // 2
    scaling = 1.0 / math.sqrt(feature)
    dma = pltpu.SemaphoreType.DMA

    local = jnp.arange(blocks, dtype=jnp.int32)
    vacant = selected == (me * blocks + local)[:, None]
    owners = selected // blocks
    inside = selected % blocks
    distant = (owners != me) & jnp.logical_not(vacant)
    near = (owners == me) & jnp.logical_not(vacant)
    peers = jnp.arange(n, dtype=jnp.int32)
    hits = distant[:, :, None] & (owners[:, :, None] == peers)
    wanted = jnp.max(jnp.where(hits, inside[:, :, None], -1), axis=(0, 1))
    nz = n // 4
    ask = jnp.broadcast_to(wanted.astype(F32).reshape(nz, 4).T[:, :, None], (4, nz, 128))
    column = owners % 4 == me % 4
    cidx = jnp.where(column, owners // 4 * 4 + inside, n + owners)
    cidx = jnp.where(vacant, me // 4 * 4 + local[:, None], cidx)
    near_hits = near[:, :, None] & (inside[:, :, None] == local)
    tcol = jnp.arange(3, dtype=jnp.int32)[None, :, None]
    far_t = jnp.min(jnp.where(hits, tcol, 4), axis=1)
    near_t = jnp.min(jnp.where(near_hits, tcol, 4), axis=1)
    near_t = jnp.where(local[:, None] == local[None, :], 3, near_t)
    tix = jnp.concatenate([far_t, near_t], axis=1).reshape(-1)
    alive = lax.dynamic_index_in_dim(
        jnp.logical_not(vacant).astype(jnp.int32), chip, 0, keepdims=False
    )
    meta = jnp.concatenate([alive, chip.astype(jnp.int32)[None]])

    q_blocks = queries.reshape(blocks, length, feature)
    do_blocks = dout.reshape(blocks, length, feature)
    k_blocks = keys.reshape(blocks, length, feature)
    v_blocks = values.reshape(blocks, length, feature)
    heads_shape = jax.ShapeDtypeStruct((4, length, feature), BF16)
    q_mine, do_mine, kv_list, asked = pl.pallas_call(
        functools.partial(fetch_kernel, nz),
        out_shape=(
            heads_shape,
            heads_shape,
            jax.ShapeDtypeStruct((3, 2, 2, 4, rows, feature), BF16),
            jax.ShapeDtypeStruct((4, nz, 128), F32),
        ),
        in_specs=[SM, VM, VM, VM, VM, VM],
        out_specs=(VM, VM, VM, VM),
        scratch_shapes=[
            pltpu.VMEM((2 * n, 2, rows, feature), BF16),
            pltpu.VMEM((3, nz, 2, rows, feature), BF16),
            pltpu.VMEM((4, 3, 2, rows, feature), BF16),
            dma((4,)),
            dma((4,)),
            dma((2, nz // 2, 2)),
            dma((nz, 2)),
            dma((3, nz)),
            dma((3, nz)),
            dma((3, 4)),
            dma((3, 4)),
            dma,
            dma,
        ],
        compiler_params=pltpu.CompilerParams(collective_id=0, has_side_effects=True),
        name="fetch",
    )(
        cidx.reshape(-1),
        ask,
        k_blocks.reshape(blocks, 8, rows, feature),
        v_blocks.reshape(blocks, 8, rows, feature),
        q_blocks,
        do_blocks,
    )
    kv_list = kv_list.reshape(3, 2, length, feature)
    per_head = pl.BlockSpec((1, length, feature), lambda h, m: (h, 0, 0))
    own_block = pl.BlockSpec((1, length, feature), lambda h, m: (m[3], 0, 0))
    gq_mine, terms = pl.pallas_call(
        functools.partial(attend_kernel, scaling),
        out_shape=(heads_shape, jax.ShapeDtypeStruct((4, 2, length, feature), BF16)),
        grid_spec=pltpu.PrefetchScalarGridSpec(
            num_scalar_prefetch=1,
            grid=(4,),
            in_specs=[
                per_head,
                per_head,
                pl.BlockSpec((3, 2, length, feature), lambda h, m: (0, 0, 0, 0)),
                own_block,
                own_block,
            ],
            out_specs=[
                per_head,
                pl.BlockSpec((4, 2, length, feature), lambda h, m: (0, 0, 0, 0)),
            ],
            scratch_shapes=[
                pltpu.VMEM((4, length, length), F32),
                pltpu.VMEM((4, length, length), F32),
                pltpu.VMEM((4, 2, length, feature), F32),
                pltpu.VMEM((4, feature, length), BF16),
            ],
        ),
        compiler_params=pltpu.CompilerParams(vmem_limit_bytes=56 * 2**20),
        name="attend",
    )(meta, q_mine, do_mine, kv_list, k_blocks, v_blocks)
    part_shape = jax.ShapeDtypeStruct((blocks, 2, 4, rows, feature), BF16)
    gq, gk, gv = pl.pallas_call(
        functools.partial(return_kernel, nz),
        out_shape=(heads_shape, part_shape, part_shape),
        in_specs=[SM, VM, VM, VM],
        out_specs=(VM, VM, VM),
        scratch_shapes=[
            pltpu.VMEM((4, 2, 4, rows, feature), BF16),
            pltpu.VMEM((4, 4, 2, rows, feature), BF16),
            pltpu.VMEM((4, 5, 2, rows, feature), BF16),
            pltpu.VMEM((4, nz, 2, rows, feature), BF16),
            pltpu.VMEM((4, nz, 2, rows, feature), BF16),
            pltpu.VMEM((nz, 2, 4, rows, feature), F32),
            pltpu.VMEM((nz, 2, 4, rows, feature), BF16),
            pltpu.VMEM((2, nz, 2, 4, rows, feature), BF16),
            pltpu.VMEM((2, 4, rows, feature), BF16),
            dma((4, nz)),
            dma((4, nz)),
            dma((nz, 2)),
            dma((2, nz, 2)),
            dma((4, 4)),
            dma((4, 4)),
            dma((3,)),
            dma((3,)),
        ],
        compiler_params=pltpu.CompilerParams(collective_id=1, has_side_effects=True),
        name="give_back",
    )(tix, terms.reshape(4, 2, 2, 4, rows, feature), gq_mine, asked)
    return (
        gq.reshape(queries.shape),
        gk.reshape(keys.shape),
        gv.reshape(values.shape),
    )


def solution(mesh):
    return jax.shard_map(
        body,
        mesh=mesh,
        in_specs=(
            P("ctx", "head", None),
            P("ctx", None),
            P("ctx", None),
            P("ctx", "head", None),
            P("ctx", None),
        ),
        out_specs=(P("ctx", "head", None), P("ctx", None), P("ctx", None)),
        check_vma=False,
    )
```

```python
import functools
import math

import jax
import jax.numpy as jnp
from jax import lax
from jax.experimental import pallas as pl
from jax.experimental.pallas import tpu as pltpu
from jax.sharding import PartitionSpec as P

MESH = pl.DeviceIdType.MESH
F32 = jnp.float32
BF16 = jnp.bfloat16
VM = pl.BlockSpec(memory_space=pltpu.VMEM)
SM = pl.BlockSpec(memory_space=pltpu.SMEM)


def place():
    me = lax.axis_index("ctx")
    head = lax.axis_index("head")
    return me // 4, me % 4, head // 2, head % 2


def greet(nz):
    z, y, chip, core = place()
    barrier = pltpu.get_barrier_semaphore()

    def hello(**where):
        pl.semaphore_signal(barrier, inc=1, device_id=where, device_id_type=MESH)

    hello(ctx=lax.rem(z + 1, nz) * 4 + y)
    hello(ctx=lax.rem(z + nz - 1, nz) * 4 + y)
    for step in range(1, 4):
        hello(ctx=z * 4 + lax.rem(y + step, 4))
        hello(head=lax.rem(chip + step, 4) * 2 + core)
    hello(head=chip * 2 + 1 - core)
    pl.semaphore_wait(barrier, 9)
    return z, y, chip, core


def kernel(
    nz,
    scaling,
    selected,
    keys,
    values,
    queries,
    dout,
    gq_out,
    gk_out,
    gv_out,
    ask,
    asked,
    pool,
    send,
    comp,
    near_kv,
    qs,
    dos,
    expo,
    dprobs,
    own_stats,
    stats,
    turned,
    gq_sum,
    gqs,
    terms,
    pair,
    outgoing,
    incoming,
    own_in,
    y_out,
    y_in,
    sums,
    z_out,
    z_in,
    final,
    ask_send,
    ask_recv,
    z_send,
    z_recv,
    y_send,
    y_recv,
    x_send,
    x_recv,
    core_send,
    core_recv,
    back_y_send,
    back_y_recv,
    back_z_send,
    back_z_recv,
):
    rows, feature = keys.shape[2:]
    length = 8 * rows
    n = 4 * nz
    reach = nz // 2
    wrap = nz - 1 - reach
    factor = scaling * math.log2(math.e)
    nt = (((1,), (1,)), ((), ()))
    z, y, chip, core = place()
    me = 4 * z + y
    part = core * 4 + chip

    cidx, code, tiles = [], [], [None] * 4
    spot = 4 * lax.broadcasted_iota(jnp.int32, (nz, 128), 0)
    for x in range(4):
        for t in range(3):
            named = selected[x, t]
            owner = lax.div(named, 4)
            inside = named - 4 * owner
            vacant = named == 4 * me + x
            plane = lax.div(owner, 4)
            seat = jnp.where(owner - 4 * plane == y, 4 * plane + inside, n + owner)
            cidx.append(jnp.where(vacant, 4 * z + x, seat))
            code.append(jnp.where(vacant, -1, jnp.where(owner == me, n + inside, owner)))
            for peer in range(4):
                tile = jnp.where(spot + peer == code[-1], inside, -1)
                tiles[peer] = tile if tiles[peer] is None else jnp.maximum(tiles[peer], tile)
    for peer in range(4):
        ask[peer] = tiles[peer].astype(F32)
    for b in range(4):
        pool[4 * z + b, 0] = keys[b, part]
        pool[4 * z + b, 1] = values[b, part]
    greet(nz)

    def to_chip(step, slot, src, dst):
        peer = lax.rem(chip + step, 4)
        return pltpu.make_async_remote_copy(
            src_ref=src(peer),
            dst_ref=dst,
            send_sem=x_send.at[slot, step],
            recv_sem=x_recv.at[slot, step],
            device_id={"head": peer * 2 + core},
            device_id_type=MESH,
        )

    def to_core(slot, src, dst):
        return pltpu.make_async_remote_copy(
            src_ref=src,
            dst_ref=dst,
            send_sem=core_send.at[slot],
            recv_sem=core_recv.at[slot],
            device_id={"head": chip * 2 + 1 - core},
            device_id_type=MESH,
        )

    def ask_copy(step):
        peer = lax.rem(y + step, 4)
        return pltpu.make_async_remote_copy(
            src_ref=ask.at[peer],
            dst_ref=asked.at[y],
            send_sem=ask_send.at[step],
            recv_sem=ask_recv.at[step],
            device_id={"ctx": z * 4 + peer},
            device_id_type=MESH,
        )

    def relay(source, half, back, hop):
        there = pool.at[pl.ds(4 * source, 4), half]
        if hop == 1:
            here = (keys, values)[half].at[:, part]
        else:
            here = there
        peer = lax.rem(z + nz - 1, nz) if back else lax.rem(z + 1, nz)
        return pltpu.make_async_remote_copy(
            src_ref=here,
            dst_ref=there,
            send_sem=z_send.at[back, hop - 1, half],
            recv_sem=z_recv.at[source, half],
            device_id={"ctx": peer * 4 + y},
            device_id_type=MESH,
        )

    def forward_source(hop):
        return z - hop + 1, jnp.logical_and(z <= nz - 2, z >= hop - 1)

    def backward_source(hop):
        source = lax.rem(z + hop - 1, nz)
        return source, source <= wrap - 1

    def start_relay(back, hop, half):
        source, needed = (backward_source if back else forward_source)(hop)

        @pl.when(needed)
        def _():
            relay(source, half, back, hop).start()

    def slot_copy(step, source):
        peer = lax.rem(y + step, 4)
        return pltpu.make_async_remote_copy(
            src_ref=send.at[step - 1, source],
            dst_ref=pool.at[4 * nz + 4 * source + y],
            send_sem=y_send.at[step - 1, source],
            recv_sem=y_recv.at[step - 1, source],
            device_id={"ctx": z * 4 + peer},
            device_id_type=MESH,
        )

    def serve(source):
        for step in range(1, 4):
            peer = lax.rem(y + step, 4)
            wish = jnp.broadcast_to(asked[peer, pl.ds(source, 1)], (16, 128))
            masks = [jnp.where(wish == b, 1.0, 0.0).astype(BF16) for b in range(4)]
            for half in range(2):
                for g in range(rows // 16):
                    span = pl.ds(16 * g, 16)
                    total = pool[4 * source, half, span] * masks[0]
                    for b in range(1, 4):
                        total = total + pool[4 * source + b, half, span] * masks[b]
                    send[step - 1, source, half, span] = total
        for step in range(1, 4):
            slot_copy(step, source).start()

    def key_rows(t):
        block = near_kv[t, 0] if t < 3 else keys[chip]
        return block.reshape(length, feature)

    def value_rows(t):
        block = near_kv[t, 1] if t < 3 else values[chip]
        return block.reshape(length, feature)

    def attend_own(h):
        s = lax.dot_general(key_rows(3), qs[h], nt, preferred_element_type=F32)
        col = lax.broadcasted_iota(jnp.int32, (length, length), 0)
        row = lax.broadcasted_iota(jnp.int32, (length, length), 1)
        s = jnp.where(col <= row, s, -jnp.inf)
        top = jnp.max(s, axis=0, keepdims=True) * factor
        e = jnp.exp2(s * factor - top)
        dp = lax.dot_general(value_rows(3), dos[h], nt, preferred_element_type=F32)
        expo[h, 3] = e
        dprobs[h, 3] = dp
        own_stats[h, 0] = top
        own_stats[h, 1] = jnp.sum(e, axis=0, keepdims=True)
        own_stats[h, 2] = jnp.sum(e * dp, axis=0, keepdims=True)

    live = [selected[chip, t] != 4 * me + chip for t in range(3)]

    def attend_far(h):
        q, do = qs[h], dos[h]
        top = own_stats[h, 0]
        for t in range(3):
            s = lax.dot_general(key_rows(t), q, nt, preferred_element_type=F32)
            expo[h, t] = s
            best = jnp.max(s, axis=0, keepdims=True) * factor
            top = jnp.maximum(top, jnp.where(live[t], best, -jnp.inf))
        shrink = jnp.exp2(own_stats[h, 0] - top)
        total = own_stats[h, 1] * shrink
        weighted = own_stats[h, 2] * shrink
        for t in range(3):
            e = jnp.exp2(expo[h, t] * factor - jnp.where(live[t], top, jnp.inf))
            dp = lax.dot_general(value_rows(t), do, nt, preferred_element_type=F32)
            total = total + jnp.sum(e, axis=0, keepdims=True)
            weighted = weighted + jnp.sum(e * dp, axis=0, keepdims=True)
            expo[h, t] = e
            dprobs[h, t] = dp
        inverse = 1.0 / total
        stats[h, 0] = inverse
        stats[h, 1] = inverse * shrink
        stats[h, 2] = weighted * inverse

    def grads(t):
        turn = turned[t]
        grad_k = grad_v = None
        for h in range(4):
            q, do = qs[h], dos[h]
            p = expo[h, t] * stats[h, 1 if t == 3 else 0]
            ds = (p * (dprobs[h, t] - stats[h, 2])).astype(BF16)
            v = jnp.dot(p.astype(BF16), do, preferred_element_type=F32)
            k = jnp.dot(ds, q, preferred_element_type=F32)
            g = jnp.dot(turn, ds, preferred_element_type=F32)
            grad_v = v if h == 0 else grad_v + v
            grad_k = k if h == 0 else grad_k + k
            if t == 0:
                gq_sum[h] = g
            elif t < 3:
                gq_sum[h] += g
            else:
                gqs[h] = ((gq_sum[h] + g) * scaling).T.astype(BF16)
        terms[t, 0] = (grad_k * scaling).astype(BF16).reshape(2, 4, rows, feature)
        terms[t, 1] = grad_v.astype(BF16).reshape(2, 4, rows, feature)

    asks = [ask_copy(step) for step in range(1, 4)]
    for copy in asks:
        copy.start()
    for half in range(2):
        start_relay(0, 1, half)
        start_relay(1, 1, half)
    q_copies = {}
    for step in (1, 3, 2):
        q_copies[step] = (
            to_chip(step, 0, lambda peer: queries.at[peer], qs.at[chip]),
            to_chip(step, 1, lambda peer: dout.at[peer], dos.at[chip]),
        )
        for copy in q_copies[step]:
            copy.start()
    asked[y] = ask[y]
    qs[chip] = queries[chip]
    dos[chip] = dout[chip]
    for copy in asks:
        copy.wait_recv()
    serve(z)

    def attend_arrived(step):
        for copy in q_copies[step]:
            copy.wait_recv()
        attend_own(lax.rem(chip + 4 - step, 4))

    for hop in range(1, reach + 1):
        near = z - hop
        far = lax.rem(z + hop, nz)
        for half in range(2):

            @pl.when(near >= 0)
            def _():
                relay(near, half, 0, 2).wait_recv()

            if hop < reach:
                start_relay(0, hop + 1, half)
            if hop <= wrap:

                @pl.when(far <= wrap - 1)
                def _():
                    relay(far, half, 1, 2).wait_recv()

                if hop < wrap:
                    start_relay(1, hop + 1, half)

        @pl.when(near >= 0)
        def _():
            serve(near)

        if hop <= wrap:

            @pl.when(jnp.logical_and(far <= wrap - 1, far < z))
            def _():
                serve(far)

        if hop == 1:
            attend_own(chip)
            turned[3] = key_rows(3).T
        elif hop == reach - 1:
            attend_arrived(1)
    attend_arrived(3)

    def got_slots(source, carry):
        for step in range(1, 4):
            slot_copy(step, source).wait_recv()
        return carry

    lax.fori_loop(0, z + 1, got_slots, 0)

    for x in range(4):
        for t in range(3):
            comp[x, t] = pool[cidx[x * 3 + t]]
    kv_copies = {
        step: to_chip(step, 2, lambda peer: comp.at[peer], near_kv.at[:, :, core, chip])
        for step in (1, 3, 2)
    }
    for copy in kv_copies.values():
        copy.start()
    for t in range(3):
        for half in range(2):
            near_kv[t, half, core, chip] = comp[chip, t, half]
    swaps = [to_core(0, comp.at[chip], near_kv.at[:, :, core, chip])]
    swaps[0].start()
    attend_arrived(2)
    for step, copy in kv_copies.items():
        copy.wait_recv()
        piece = near_kv.at[:, :, core, lax.rem(chip + 4 - step, 4)]
        swaps.append(to_core(step, piece, piece))
        swaps[-1].start()
    for x in range(4):
        incoming[x, 3] = jnp.zeros_like(incoming[x, 3])
    for owner in range(nz):
        sums[owner] = jnp.zeros_like(sums[owner])
    for copy in swaps:
        copy.wait_recv()

    for t in range(3):
        turned[t] = key_rows(t).T

    def far_head(h, carry):
        attend_far(h)
        return carry

    lax.fori_loop(0, 4, far_head, 0)

    merges = [to_core(4 + t, terms.at[t, :, 1 - core], pair.at[t]) for t in range(4)]

    def spread_copies(t):
        there = own_in.at[chip] if t == 3 else incoming.at[chip, t]
        return [to_chip(step, 3 + t, lambda peer: outgoing.at[peer, t], there) for step in (1, 3, 2)]

    spreads = [spread_copies(t) for t in range(4)]

    def combine(t):
        merges[t].wait_recv()
        for half in range(2):
            for x in range(4):
                total = terms[t, half, core, x].astype(F32) + pair[t, half, x].astype(F32)
                outgoing[x, t, half] = total.astype(BF16)
        for copy in spreads[t]:
            copy.start()
        if t == 3:
            own_in[chip] = outgoing[chip, t]
        else:
            incoming[chip, t] = outgoing[chip, t]

    for t in range(3):
        grads(t)
        merges[t].start()
        if t > 0:
            combine(t - 1)
    combine(2)
    grads(3)
    merges[3].start()
    gq_copies = [
        to_chip(step, 7, lambda peer: gqs.at[peer], gq_out.at[chip]) for step in (1, 3, 2)
    ]
    for t in range(3):
        for copy in spreads[t]:
            copy.wait_recv()

    def give_copy(step, owner):
        return pltpu.make_async_remote_copy(
            src_ref=y_out.at[step, owner],
            dst_ref=y_in.at[step, owner],
            send_sem=back_y_send.at[step, owner],
            recv_sem=back_y_recv.at[step, owner],
            device_id={"ctx": z * 4 + lax.rem(y + step, 4)},
            device_id_type=MESH,
        )

    def reduce_copy(owner, half, back):
        peer = lax.rem(z + 1, nz) if back else lax.rem(z + nz - 1, nz)
        return pltpu.make_async_remote_copy(
            src_ref=z_out.at[owner, half],
            dst_ref=z_in.at[back, owner, half],
            send_sem=back_z_send.at[owner, half],
            recv_sem=back_z_recv.at[back, owner, half],
            device_id={"ctx": peer * 4 + y},
            device_id_type=MESH,
        )

    def collect(spot):
        total = None
        for x in range(4):
            which = 3
            for t in range(3):
                which = jnp.where(code[3 * x + t] == spot, t, which)
            term = incoming[x, which].astype(F32)
            total = term if total is None else total + term
        return total

    def give(owner):
        for step in range(4):
            y_out[step, owner] = collect(4 * owner + lax.rem(y + step, 4)).astype(BF16)
        for step in range(1, 4):
            give_copy(step, owner).start()

    def gather(owner):
        for step in range(1, 4):
            give_copy(step, owner).wait_recv()
        masks = []
        for step in range(4):
            wish = jnp.broadcast_to(asked[lax.rem(y + 4 - step, 4), pl.ds(owner, 1)], (16, 128))
            masks.append([jnp.where(wish == b, 1.0, 0.0) for b in range(4)])
        for half in range(2):
            for g in range(rows // 16):
                span = pl.ds(16 * g, 16)
                parts = [y_out[0, owner, half, span].astype(F32)]
                for step in range(1, 4):
                    parts.append(y_in[step, owner, half, span].astype(F32))
                for b in range(4):
                    total = parts[0] * masks[0][b]
                    for step in range(1, 4):
                        total = total + parts[step] * masks[step][b]
                    sums[owner, half, b, span] = total

    def pass_on(owner, half, back, last):
        if last:
            z_out[owner, half] = sums[owner, half].astype(BF16)
        elif back:
            reduce_copy(owner, half, back).wait_recv()
            z_out[owner, half] = (
                sums[owner, half] + z_in[back, owner, half].astype(F32)
            ).astype(BF16)
        else:

            @pl.when(z <= nz - 2)
            def _():
                reduce_copy(owner, half, back).wait_recv()
                z_out[owner, half] = (
                    sums[owner, half] + z_in[back, owner, half].astype(F32)
                ).astype(BF16)

            @pl.when(z == nz - 1)
            def _():
                z_out[owner, half] = sums[owner, half].astype(BF16)

        reduce_copy(owner, half, back).start()

    steps = []
    for i in range(reach):
        near = z - (reach - i)
        steps.append((near, near >= 0, near >= 0, 0, i == 0))
        if i < wrap:
            far = lax.rem(z + wrap - i, nz)
            needed = far <= wrap - 1
            steps.append((far, needed, jnp.logical_and(needed, far < z), 1, i == 0))
    for owner, _, mine, _, _ in steps:

        @pl.when(mine)
        def _():
            give(owner)

    give(z)
    combine(3)
    for copy in gq_copies:
        copy.start()
    gq_out[chip] = gqs[chip]
    for owner, needed, mine, back, last in steps:

        @pl.when(mine)
        def _():
            gather(owner)

        @pl.when(needed)
        def _():
            for half in range(2):
                pass_on(owner, half, back, last)

    gather(z)
    for copy in spreads[3]:
        copy.wait_recv()
    for b in range(4):
        near_sum = collect(n + b) + own_in[b].astype(F32)
        for half in range(2):
            sums[z, half, b] += near_sum[half]
    shares, tails = {}, []
    outs = (gk_out, gv_out)
    for half in range(2):

        @pl.when(z <= nz - 2)
        def _():
            reduce_copy(z, half, 0).wait_recv()
            sums[z, half] += z_in[0, z, half].astype(F32)

        @pl.when(z <= wrap - 1)
        def _():
            reduce_copy(z, half, 1).wait_recv()
            sums[z, half] += z_in[1, z, half].astype(F32)

        final[half] = sums[z, half].astype(BF16)
        for step in (1, 3, 2):
            copy = to_chip(step, 8 + half, lambda peer: final.at[half], outs[half].at[:, core, chip])
            copy.start()
            shares[half, step] = copy
        tails.append(to_core(8 + 4 * half, final.at[half], outs[half].at[:, core, chip]))
        tails[-1].start()
        for b in range(4):
            outs[half][b, core, chip] = final[half, b]
    for half in range(2):
        for step in (1, 3, 2):
            shares[half, step].wait_recv()
            piece = outs[half].at[:, core, lax.rem(chip + 4 - step, 4)]
            tails.append(to_core(8 + 4 * half + step, piece, piece))
            tails[-1].start()

    for copy in asks + list(kv_copies.values()) + swaps + merges + list(shares.values()):
        copy.wait_send()
    for pairs in q_copies.values():
        for copy in pairs:
            copy.wait_send()
    for t in range(4):
        for copy in spreads[t]:
            copy.wait_send()
    for back, last in ((0, reach), (1, wrap)):
        for hop in range(1, last + 1):
            source, needed = (backward_source if back else forward_source)(hop)
            for half in range(2):

                @pl.when(needed)
                def _():
                    relay(source, half, back, hop).wait_send()

    for owner, needed, _, back, _ in steps:

        @pl.when(needed)
        def _():
            for half in range(2):
                reduce_copy(owner, half, back).wait_send()

    def sent_slots(owner, carry):
        for step in range(1, 4):
            slot_copy(step, owner).wait_send()
            give_copy(step, owner).wait_send()
        return carry

    lax.fori_loop(0, z + 1, sent_slots, 0)
    for copy in gq_copies + tails:
        copy.wait()


def body(queries, keys, values, dout, selected):
    tok, _, feature = queries.shape
    blocks = selected.shape[0]
    length = tok // blocks
    rows = length // 8
    n = lax.axis_size("ctx")
    nz = n // 4
    scaling = 1.0 / math.sqrt(feature)
    dma = pltpu.SemaphoreType.DMA
    heads = (4, length, feature)
    slab = (rows, feature)
    part_shape = jax.ShapeDtypeStruct((blocks, 2, 4, *slab), BF16)
    gq, gk, gv = pl.pallas_call(
        functools.partial(kernel, nz, scaling),
        out_shape=(jax.ShapeDtypeStruct(heads, BF16), part_shape, part_shape),
        in_specs=[SM, VM, VM, VM, VM],
        out_specs=(VM, VM, VM),
        scratch_shapes=[
            pltpu.VMEM((4, nz, 128), F32),
            pltpu.VMEM((4, nz, 128), F32),
            pltpu.VMEM((2 * n, 2, *slab), BF16),
            pltpu.VMEM((3, nz, 2, *slab), BF16),
            pltpu.VMEM((4, 3, 2, *slab), BF16),
            pltpu.VMEM((3, 2, 2, 4, *slab), BF16),
            pltpu.VMEM(heads, BF16),
            pltpu.VMEM(heads, BF16),
            pltpu.VMEM((4, 4, length, length), F32),
            pltpu.VMEM((4, 4, length, length), F32),
            pltpu.VMEM((4, 3, 1, length), F32),
            pltpu.VMEM((4, 3, 1, length), F32),
            pltpu.VMEM((4, feature, length), BF16),
            pltpu.VMEM((4, feature, length), F32),
            pltpu.VMEM(heads, BF16),
            pltpu.VMEM((4, 2, 2, 4, *slab), BF16),
            pltpu.VMEM((4, 2, 4, *slab), BF16),
            pltpu.VMEM((4, 4, 2, *slab), BF16),
            pltpu.VMEM((4, 4, 2, *slab), BF16),
            pltpu.VMEM((4, 2, *slab), BF16),
            pltpu.VMEM((4, nz, 2, *slab), BF16),
            pltpu.VMEM((4, nz, 2, *slab), BF16),
            pltpu.VMEM((nz, 2, 4, *slab), F32),
            pltpu.VMEM((nz, 2, 4, *slab), BF16),
            pltpu.VMEM((2, nz, 2, 4, *slab), BF16),
            pltpu.VMEM((2, 4, *slab), BF16),
            dma((4,)),
            dma((4,)),
            dma((2, nz // 2, 2)),
            dma((nz, 2)),
            dma((3, nz)),
            dma((3, nz)),
            dma((10, 4)),
            dma((10, 4)),
            dma((16,)),
            dma((16,)),
            dma((4, nz)),
            dma((4, nz)),
            dma((nz, 2)),
            dma((2, nz, 2)),
        ],
        compiler_params=pltpu.CompilerParams(
            collective_id=0, has_side_effects=True, vmem_limit_bytes=62 * 2**20
        ),
        name="whole",
    )(
        selected,
        keys.reshape(blocks, 8, *slab),
        values.reshape(blocks, 8, *slab),
        queries.reshape(heads),
        dout.reshape(heads),
    )
    return (
        gq.reshape(queries.shape),
        gk.reshape(keys.shape),
        gv.reshape(values.shape),
    )


def solution(mesh):
    return jax.shard_map(
        body,
        mesh=mesh,
        in_specs=(
            P("ctx", "head", None),
            P("ctx", None),
            P("ctx", None),
            P("ctx", "head", None),
            P("ctx", None),
        ),
        out_specs=(P("ctx", "head", None), P("ctx", None), P("ctx", None)),
        check_vma=False,
    )
```
